32 devices in a mesh: dp: 8 (over y, x, core), group: 4 (over z).
Axes of the slice: x: 2, y: 2, z: 4, core: 2. Of those that a mesh axis runs over, the one named last changes fastest.
Arguments:
- stream: float32 [8192, 1024], P(('dp', 'group')), may hold values from -6 to 6
- cotangent: float32 [8192, 1024], P(('dp', 'group')), may hold values from -6 to 6
- bounds: int32 [8192, 2], P(('dp', 'group')), may hold values from 0 to 8192, as said below
- joined_proj: float32 [1024, 3072], P(('dp', 'group'))
- out_proj: float32 [1024, 1024], P(('dp', 'group')), may hold values from -3 to 3
- wide_proj: float32 [1024, 5248], P(('dp', 'group')), may hold values from -0.1875 to 0.1875
- down_proj: float32 [1024, 2624], P(('dp', 'group')), may hold values from -0.125 to 0.125
- gain_first: float32 [1024], P(('dp', 'group')), may hold values from 0.5 to 1.5
- gain_second: float32 [1024], P(('dp', 'group')), may hold values from 0.5 to 1.5
- joined_momentum: float32 [1024, 3072], P(('dp', 'group')), may hold values from -6 to 6
- out_momentum: float32 [1024, 1024], P(('dp', 'group')), may hold values from -6 to 6
- wide_momentum: float32 [1024, 5248], P(('dp', 'group')), may hold values from -6 to 6
- down_momentum: float32 [1024, 2624], P(('dp', 'group')), may hold values from -6 to 6
- gain_first_momentum: float32 [1024], P(('dp', 'group')), may hold values from -6 to 6
- gain_second_momentum: float32 [1024], P(('dp', 'group')), may hold values from -6 to 6
- joined_variance: float32 [1024, 3072], P(('dp', 'group')), may hold values from 1 to 100
- out_variance: float32 [1024, 1024], P(('dp', 'group')), may hold values from 1 to 100
- wide_variance: float32 [1024, 5248], P(('dp', 'group')), may hold values from 1 to 100
- down_variance: float32 [1024, 2624], P(('dp', 'group')), may hold values from 1 to 100
- gain_first_variance: float32 [1024], P(('dp', 'group')), may hold values from 1 to 100
- gain_second_variance: float32 [1024], P(('dp', 'group')), may hold values from 1 to 100
Outputs:
- output: float32 [8192, 1024], P(('dp', 'group'))
- stream_grad: float32 [8192, 1024], P(('dp', 'group'))
- joined_grad: float32 [1024, 3072], P(('dp', 'group'))
- out_grad: float32 [1024, 1024], P(('dp', 'group'))
- wide_grad: float32 [1024, 5248], P(('dp', 'group'))
- down_grad: float32 [1024, 2624], P(('dp', 'group'))
- gain_first_grad: float32 [1024], P(('dp', 'group'))
- gain_second_grad: float32 [1024], P(('dp', 'group'))
- joined_new: float32 [1024, 3072], P(('dp', 'group'))
- out_new: float32 [1024, 1024], P(('dp', 'group'))
- wide_new: float32 [1024, 5248], P(('dp', 'group'))
- down_new: float32 [1024, 2624], P(('dp', 'group'))
- gain_first_new: float32 [1024], P(('dp', 'group'))
- gain_second_new: float32 [1024], P(('dp', 'group'))
- joined_momentum_new: float32 [1024, 3072], P(('dp', 'group'))
- out_momentum_new: float32 [1024, 1024], P(('dp', 'group'))
- wide_momentum_new: float32 [1024, 5248], P(('dp', 'group'))
- down_momentum_new: float32 [1024, 2624], P(('dp', 'group'))
- gain_first_momentum_new: float32 [1024], P(('dp', 'group'))
- gain_second_momentum_new: float32 [1024], P(('dp', 'group'))
- joined_variance_new: float32 [1024, 3072], P(('dp', 'group'))
- out_variance_new: float32 [1024, 1024], P(('dp', 'group'))
- wide_variance_new: float32 [1024, 5248], P(('dp', 'group'))
- down_variance_new: float32 [1024, 2624], P(('dp', 'group'))
- gain_first_variance_new: float32 [1024], P(('dp', 'group'))
- gain_second_variance_new: float32 [1024], P(('dp', 'group'))
The draws below stay inside these ranges and needn't reach their ends.
Inputs may be any that keep to these rules, and one draw needn't show every extreme that they name: `bounds`: each row holds the first token index and one past the last token index of that token's sequence; sequences are contiguous, cover all tokens in order and hold 1 to 1024 tokens, exactly 1024 for one of them, 128 or more for all but the last.
All inputs are finite; a program needn't handle non-finite values.
Results may differ from the reference program's by a relative error of at most 0.018.
Values may be sent and summed in bfloat16 or wider, within the bound.
A program may use at most 320 MiB of HBM per device.

```python
import math
import jax
import jax.numpy as jnp
from jax import lax

D = 1024
HEAD_DIM = 64
FF = 2624
LMAX = 1024
LMIN = 128
STEP = 4
TOKENS = 8192


def draw_bounds(key, part):
    count = TOKENS // LMIN + 1
    lengths = jax.random.randint(jax.random.fold_in(key, 21), (count,), LMIN, LMAX + 1)
    chosen_seq = jax.random.randint(jax.random.fold_in(key, 22), (), 0, 8)
    lengths = jnp.where(jnp.arange(count) == chosen_seq, LMAX, lengths)
    seq_ends = jnp.cumsum(lengths)
    seq_starts = seq_ends - lengths
    token_index = jnp.arange(TOKENS)
    owner = jnp.sum((seq_ends[None, :] <= token_index[:, None]).astype(jnp.int32), axis=1)
    first_token = jnp.take(seq_starts, owner)
    last_token = jnp.minimum(jnp.take(seq_ends, owner), TOKENS)
    return jnp.stack([first_token, last_token], axis=1).astype(jnp.int32)


def draw_joined_proj(key, part):
    base = jax.random.normal(jax.random.fold_in(key, 11), (D, 3 * D), jnp.float32) * D ** (-0.5)
    return base


def steps_of(rng, extent, shards, low, top_value):
    gain = 1.0
    for dim, blocks in shards:
        heights = jax.random.uniform(jax.random.fold_in(jax.random.fold_in(rng, 6), dim), (blocks,), jnp.float32, low / len(shards), top_value / len(shards))
        gain = gain * jnp.repeat(jnp.exp(heights), extent[dim] // blocks).reshape((-1,) + (1,) * (len(extent) - 1 - dim))
    return gain


def bell_draw(stream_key, shape, scale, bound, pieces=(), kind=jnp.bfloat16):
    factor_of = steps_of(stream_key, shape, pieces, -0.22, 0.18) if pieces else 1.0
    drawn = jax.random.normal(stream_key, shape, jnp.float32) * scale * factor_of
    return jnp.minimum(jnp.maximum(drawn, -bound), bound).astype(kind)


def setup_inputs(seed: int = 0) -> dict:
    seeds = jax.random.split(jax.random.key(seed), 22)
    stream = bell_draw(seeds[0], (TOKENS, D), 1.0, 6.0, ((0, 32),), jnp.float32)
    cotangent = bell_draw(seeds[1], (TOKENS, D), 1.0, 6.0, ((0, 32),), jnp.float32)
    bounds = draw_bounds(jax.random.fold_in(seeds[21], 71), 0)
    joined_proj = draw_joined_proj(jax.random.fold_in(seeds[21], 71), 0)
    out_proj = bell_draw(seeds[4], (D, D), (max(D // 256, 1)) ** -0.5, 3.0, ((0, 32),), jnp.float32)
    wide_proj = bell_draw(seeds[5], (D, 2 * FF), D ** -0.5, 0.1875, ((0, 32),), jnp.float32)
    down_proj = bell_draw(seeds[6], (D, FF), FF ** -0.5, 0.125, ((0, 32),), jnp.float32)
    gain_first = jnp.clip(1.0 + 0.1 * jax.random.normal(seeds[7], (D,), jnp.float32), 0.5, 1.5)
    gain_second = jnp.clip(1.0 + 0.1 * jax.random.normal(seeds[8], (D,), jnp.float32), 0.5, 1.5)
    joined_momentum = bell_draw(seeds[9], (D, 3 * D), 1.0, 6.0, ((0, 32),), jnp.float32)
    out_momentum = bell_draw(seeds[10], (D, D), 1.0, 6.0, ((0, 32),), jnp.float32)
    wide_momentum = bell_draw(seeds[11], (D, 2 * FF), 1.0, 6.0, ((0, 32),), jnp.float32)
    down_momentum = bell_draw(seeds[12], (D, FF), 1.0, 6.0, ((0, 32),), jnp.float32)
    gain_first_momentum = bell_draw(seeds[13], (D,), 1.0, 6.0, ((0, 32),), jnp.float32)
    gain_second_momentum = bell_draw(seeds[14], (D,), 1.0, 6.0, ((0, 32),), jnp.float32)
    joined_variance = jnp.clip(jnp.exp(math.log(100.0) - 4.6051702 * jax.random.uniform(seeds[15], (D, 3 * D), jnp.float32) ** steps_of(seeds[15], (D, 3 * D), ((0, 32),), -0.2, 0.2)), 1.0, 100.0)
    out_variance = jnp.clip(jnp.exp(math.log(100.0) - 4.6051702 * jax.random.uniform(seeds[16], (D, D), jnp.float32) ** steps_of(seeds[16], (D, D), ((0, 32),), -0.2, 0.2)), 1.0, 100.0)
    wide_variance = jnp.clip(jnp.exp(math.log(100.0) - 4.6051702 * jax.random.uniform(seeds[17], (D, 2 * FF), jnp.float32) ** steps_of(seeds[17], (D, 2 * FF), ((0, 32),), -0.2, 0.2)), 1.0, 100.0)
    down_variance = jnp.clip(jnp.exp(math.log(100.0) - 4.6051702 * jax.random.uniform(seeds[18], (D, FF), jnp.float32) ** steps_of(seeds[18], (D, FF), ((0, 32),), -0.2, 0.2)), 1.0, 100.0)
    gain_first_variance = jnp.clip(jnp.exp(math.log(100.0) - 4.6051702 * jax.random.uniform(seeds[19], (D,), jnp.float32) ** steps_of(seeds[19], (D,), ((0, 32),), -0.2, 0.2)), 1.0, 100.0)
    gain_second_variance = jnp.clip(jnp.exp(math.log(100.0) - 4.6051702 * jax.random.uniform(seeds[20], (D,), jnp.float32) ** steps_of(seeds[20], (D,), ((0, 32),), -0.2, 0.2)), 1.0, 100.0)
    return dict(stream=stream, cotangent=cotangent, bounds=bounds, joined_proj=joined_proj, out_proj=out_proj, wide_proj=wide_proj, down_proj=down_proj, gain_first=gain_first, gain_second=gain_second, joined_momentum=joined_momentum, out_momentum=out_momentum, wide_momentum=wide_momentum, down_momentum=down_momentum, gain_first_momentum=gain_first_momentum, gain_second_momentum=gain_second_momentum, joined_variance=joined_variance, out_variance=out_variance, wide_variance=wide_variance, down_variance=down_variance, gain_first_variance=gain_first_variance, gain_second_variance=gain_second_variance)


EPSILON = 1e-05
ROPE_BASE = 160000.0
LEARN_RATE = 0.02
BETA_ONE = 0.9
BETA_TWO = 0.98
ADAM_EPSILON = 1e-06
WEIGHT_DECAY = 0.1
NEG_LARGE = -1e+30

def normalize(values):
    centred = values - lax.optimization_barrier(jnp.mean(values, axis=1, keepdims=True))
    row_scale = lax.rsqrt(lax.optimization_barrier(jnp.mean(centred * centred, axis=1, keepdims=True)) + EPSILON)
    return (centred * row_scale, row_scale)

def norm_back(grad_hat, normed, row_scale):
    mean_one = lax.optimization_barrier(jnp.mean(grad_hat, axis=1, keepdims=True))
    mean_two = lax.optimization_barrier(jnp.mean(grad_hat * normed, axis=1, keepdims=True))
    return row_scale * (grad_hat - mean_one - normed * mean_two)

def rope_tables(positions):
    half_dim = HEAD_DIM // 2
    freqs = jnp.exp(jnp.arange(half_dim, dtype=jnp.float32) * (-2.0 * math.log(ROPE_BASE) / HEAD_DIM))
    angles = positions.astype(jnp.float32)[:, None] * freqs[None, :]
    return (jnp.cos(angles), jnp.sin(angles))

def rotate(values, cosine, sine_table, sign):
    half_dim = values.shape[-1] // 2
    front_half = values[..., :half_dim]
    second = values[..., half_dim:]
    cos_part = cosine[:, None, :]
    sin_part = sine_table[:, None, :] * sign
    return jnp.concatenate([front_half * cos_part - second * sin_part, second * cos_part + front_half * sin_part], axis=-1)

def gelu_parts(inner_part):
    cdf_part = 0.5 * (1.0 + lax.erf(inner_part * (1.0 / math.sqrt(2.0))))
    activation = inner_part * cdf_part
    gelu_slope = cdf_part + inner_part * jnp.exp(-0.5 * inner_part * inner_part) * (1.0 / math.sqrt(2.0 * math.pi))
    return (activation, gelu_slope)

def score_block(queries, win_keys, key_mask):
    scores = jnp.einsum('rhd,khd->hrk', queries.astype(jnp.float32), win_keys.astype(jnp.float32)) * HEAD_DIM ** (-0.5)
    return jnp.where(key_mask[None], scores, NEG_LARGE)

def attend_forward(queries, win_keys, win_values, key_mask):
    scores = score_block(queries, win_keys, key_mask)
    row_peak = lax.optimization_barrier(jnp.max(scores, axis=2, keepdims=True))
    sum_exp = lax.optimization_barrier(jnp.sum(jnp.exp(scores - row_peak), axis=2, keepdims=True))
    log_norm = row_peak + jnp.log(sum_exp)
    prob_round = jnp.exp(scores - log_norm).astype(jnp.bfloat16)
    mixed = jnp.einsum('hrk,khd->rhd', prob_round.astype(jnp.float32), win_values.astype(jnp.float32))
    return (mixed, log_norm[..., 0])

def attend_backward(queries, win_keys, win_values, key_mask, log_norm, attended, grad_attended):
    scores = score_block(queries, win_keys, key_mask)
    probs = jnp.exp(scores - log_norm[..., None])
    prob_round = probs.astype(jnp.bfloat16)
    grad_prob = jnp.einsum('rhd,khd->hrk', grad_attended.astype(jnp.float32), win_values.astype(jnp.float32))
    row_delta = lax.optimization_barrier(jnp.sum(grad_attended.astype(jnp.float32) * attended.astype(jnp.float32), axis=2)).T
    grad_score = (probs * (grad_prob - row_delta[..., None])).astype(jnp.bfloat16)
    grad_query = jnp.einsum('hrk,khd->rhd', grad_score.astype(jnp.float32), win_keys.astype(jnp.float32)) * HEAD_DIM ** (-0.5)
    grad_key = jnp.einsum('hrk,rhd->khd', grad_score.astype(jnp.float32), queries.astype(jnp.float32)) * HEAD_DIM ** (-0.5)
    grad_value = jnp.einsum('hrk,rhd->khd', prob_round.astype(jnp.float32), grad_attended.astype(jnp.float32))
    return (grad_query, grad_key, grad_value)

def adam_step(weight, gradient, momentum, variance, decay_rate):
    new_momentum = BETA_ONE * momentum + (1.0 - BETA_ONE) * gradient
    new_variance = BETA_TWO * variance + (1.0 - BETA_TWO) * gradient * gradient
    update = new_momentum / (1.0 - BETA_ONE ** STEP) / (jnp.sqrt(new_variance / (1.0 - BETA_TWO ** STEP)) + ADAM_EPSILON)
    return (weight - LEARN_RATE * (update + decay_rate * weight), new_momentum, new_variance)

def reference(stream, cotangent, bounds, joined_proj, out_proj, wide_proj, down_proj, gain_first, gain_second, joined_momentum, out_momentum, wide_momentum, down_momentum, gain_first_momentum, gain_second_momentum, joined_variance, out_variance, wide_variance, down_variance, gain_first_variance, gain_second_variance):
    joined_half = joined_proj.astype(jnp.bfloat16)
    out_half = out_proj.astype(jnp.bfloat16)
    wide_half = wide_proj.astype(jnp.bfloat16)
    down_half = down_proj.astype(jnp.bfloat16)
    gain_one = lax.optimization_barrier(gain_first.astype(jnp.bfloat16)).astype(jnp.float32)
    gain_two = lax.optimization_barrier(gain_second.astype(jnp.bfloat16)).astype(jnp.float32)
    heads = D // HEAD_DIM
    block_rows = min(4096, TOKENS)
    blocks = TOKENS // block_rows
    seq_starts = bounds[:, 0]
    seq_ends = bounds[:, 1]
    cosine, sine_table = rope_tables(jnp.arange(TOKENS, dtype=jnp.int32) - seq_starts)

    def front(block_index):
        first_row = (block_index * block_rows).astype(jnp.int32)
        row_block = lax.dynamic_slice_in_dim(stream, first_row, block_rows, 0)
        cos_block = lax.dynamic_slice_in_dim(cosine, first_row, block_rows, 0)
        sin_block = lax.dynamic_slice_in_dim(sine_table, first_row, block_rows, 0)
        normed, row_scale = normalize(row_block)
        normed_in = (normed * gain_one).astype(jnp.bfloat16)
        joined_act = jnp.dot(normed_in, joined_half, preferred_element_type=jnp.float32)
        queries = rotate(joined_act[:, :D].reshape(block_rows, heads, HEAD_DIM), cos_block, sin_block, 1.0)
        win_keys = rotate(joined_act[:, D:2 * D].reshape(block_rows, heads, HEAD_DIM), cos_block, sin_block, 1.0)
        queries = queries.astype(jnp.bfloat16).reshape(block_rows, D)
        pairs = jnp.concatenate([win_keys.astype(jnp.bfloat16).reshape(block_rows, D), joined_act[:, 2 * D:].astype(jnp.bfloat16)], axis=1)
        return (normed_in, queries, pairs)
    normed_in, queries, pairs = lax.map(front, jnp.arange(blocks, dtype=jnp.int32))
    normed_in = normed_in.reshape(TOKENS, D)
    queries = queries.reshape(TOKENS, D)
    pairs = pairs.reshape(TOKENS, 2 * D)
    query_rows = min(512, TOKENS)
    query_blocks = TOKENS // query_rows
    key_span = query_rows + 2 * LMAX
    padded = jnp.pad(pairs, ((LMAX, LMAX), (0, 0)))

    def window_of(block_index):
        first_row = (block_index * query_rows).astype(jnp.int32)
        window = lax.dynamic_slice_in_dim(padded, first_row, key_span, 0)
        key_index = first_row - LMAX + jnp.arange(key_span, dtype=jnp.int32)
        start_rows = lax.dynamic_slice_in_dim(seq_starts, first_row, query_rows, 0)
        end_rows = lax.dynamic_slice_in_dim(seq_ends, first_row, query_rows, 0)
        key_mask = (key_index[None, :] >= start_rows[:, None]) & (key_index[None, :] < end_rows[:, None])
        win_keys = window[:, :D].reshape(key_span, heads, HEAD_DIM)
        win_values = window[:, D:].reshape(key_span, heads, HEAD_DIM)
        query_block = lax.dynamic_slice_in_dim(queries, first_row, query_rows, 0).reshape(query_rows, heads, HEAD_DIM)
        return (first_row, query_block, win_keys, win_values, key_mask)

    def attend_block(block_index):
        first_row, query_block, win_keys, win_values, key_mask = window_of(block_index)
        mixed, log_norm = attend_forward(query_block, win_keys, win_values, key_mask)
        return (mixed.astype(jnp.bfloat16).reshape(query_rows, D), log_norm)
    attended, log_norms = lax.map(attend_block, jnp.arange(query_blocks, dtype=jnp.int32))
    attended = attended.reshape(TOKENS, D)

    def middle(block_index):
        first_row = (block_index * block_rows).astype(jnp.int32)
        row_block = lax.dynamic_slice_in_dim(stream, first_row, block_rows, 0)
        cot_block = lax.dynamic_slice_in_dim(cotangent, first_row, block_rows, 0)
        att_block = lax.dynamic_slice_in_dim(attended, first_row, block_rows, 0)
        residual = row_block + jnp.dot(att_block, out_half, preferred_element_type=jnp.float32)
        normed, row_scale = normalize(residual)
        hidden_in = (normed * gain_two).astype(jnp.bfloat16)
        wide_act = jnp.dot(hidden_in, wide_half, preferred_element_type=jnp.float32)
        inner_part = wide_act[:, :FF]
        gate_part = wide_act[:, FF:]
        activation, gelu_slope = gelu_parts(inner_part)
        gated = (activation * gate_part).astype(jnp.bfloat16)
        output = residual + jnp.dot(gated, down_half.T, preferred_element_type=jnp.float32)
        cot_half = cot_block.astype(jnp.bfloat16)
        down_part = jnp.dot(cot_half.T, gated, preferred_element_type=jnp.float32)
        grad_gated = jnp.dot(cot_half, down_half, preferred_element_type=jnp.float32)
        grad_wide = jnp.concatenate([grad_gated * gate_part * gelu_slope, grad_gated * activation], axis=1).astype(jnp.bfloat16)
        wide_part = jnp.dot(hidden_in.T, grad_wide, preferred_element_type=jnp.float32)
        grad_hidden = jnp.dot(grad_wide, wide_half.T, preferred_element_type=jnp.float32)
        gain_two_part = lax.optimization_barrier(jnp.sum(grad_hidden * normed, axis=0))
        grad_resid = cot_block + norm_back(grad_hidden * gain_two, normed, row_scale)
        resid_half = grad_resid.astype(jnp.bfloat16)
        out_part = jnp.dot(att_block.T, resid_half, preferred_element_type=jnp.float32)
        grad_attended = jnp.dot(resid_half, out_half.T, preferred_element_type=jnp.float32).astype(jnp.bfloat16)
        return (output, grad_resid, grad_attended, down_part, wide_part, out_part, gain_two_part)
    output, grad_resid, grad_attended, down_parts, wide_parts, out_parts, gain_two_parts = lax.map(middle, jnp.arange(blocks, dtype=jnp.int32))
    output = output.reshape(TOKENS, D)
    grad_resid = grad_resid.reshape(TOKENS, D)
    grad_attended = grad_attended.reshape(TOKENS, D)
    down_grad = lax.optimization_barrier(jnp.sum(down_parts, axis=0))
    wide_grad = lax.optimization_barrier(jnp.sum(wide_parts, axis=0))
    out_grad = lax.optimization_barrier(jnp.sum(out_parts, axis=0))
    gain_second_grad = lax.optimization_barrier(jnp.sum(gain_two_parts, axis=0))

    def back_step(accum, block_index):
        first_row, query_block, win_keys, win_values, key_mask = window_of(block_index)
        att_block = lax.dynamic_slice_in_dim(attended, first_row, query_rows, 0).reshape(query_rows, heads, HEAD_DIM)
        grad_block = lax.dynamic_slice_in_dim(grad_attended, first_row, query_rows, 0).reshape(query_rows, heads, HEAD_DIM)
        log_norm = log_norms[block_index]
        grad_query, grad_key, grad_value = attend_backward(query_block, win_keys, win_values, key_mask, log_norm, att_block, grad_block)
        grad_window = jnp.concatenate([grad_key.reshape(key_span, D), grad_value.reshape(key_span, D)], axis=1)
        current = lax.dynamic_slice_in_dim(accum, first_row, key_span, 0)
        accum = lax.dynamic_update_slice_in_dim(accum, current + grad_window, first_row, 0)
        return (accum, grad_query.reshape(query_rows, D))
    accum, grad_queries = lax.scan(back_step, jnp.zeros((TOKENS + 2 * LMAX, 2 * D), jnp.float32), jnp.arange(query_blocks, dtype=jnp.int32))
    pair_grad = accum[LMAX:LMAX + TOKENS]
    grad_queries = grad_queries.reshape(TOKENS, D)

    def rear(block_index):
        first_row = (block_index * block_rows).astype(jnp.int32)
        row_block = lax.dynamic_slice_in_dim(stream, first_row, block_rows, 0)
        cos_block = lax.dynamic_slice_in_dim(cosine, first_row, block_rows, 0)
        sin_block = lax.dynamic_slice_in_dim(sine_table, first_row, block_rows, 0)
        query_grad_block = lax.dynamic_slice_in_dim(grad_queries, first_row, block_rows, 0)
        pair_block = lax.dynamic_slice_in_dim(pair_grad, first_row, block_rows, 0)
        resid_block = lax.dynamic_slice_in_dim(grad_resid, first_row, block_rows, 0)
        normed_block = lax.dynamic_slice_in_dim(normed_in, first_row, block_rows, 0)
        normed, row_scale = normalize(row_block)
        query_back = rotate(query_grad_block.reshape(block_rows, heads, HEAD_DIM), cos_block, sin_block, -1.0)
        key_back = rotate(pair_block[:, :D].reshape(block_rows, heads, HEAD_DIM), cos_block, sin_block, -1.0)
        grad_joined = jnp.concatenate([query_back.reshape(block_rows, D), key_back.reshape(block_rows, D), pair_block[:, D:]], axis=1).astype(jnp.bfloat16)
        joined_part = jnp.dot(normed_block.T, grad_joined, preferred_element_type=jnp.float32)
        grad_normed = jnp.dot(grad_joined, joined_half.T, preferred_element_type=jnp.float32)
        gain_one_part = lax.optimization_barrier(jnp.sum(grad_normed * normed, axis=0))
        stream_part = resid_block + norm_back(grad_normed * gain_one, normed, row_scale)
        return (stream_part, joined_part, gain_one_part)
    stream_grad, joined_parts, gain_one_parts = lax.map(rear, jnp.arange(blocks, dtype=jnp.int32))
    stream_grad = stream_grad.reshape(TOKENS, D)
    joined_grad = lax.optimization_barrier(jnp.sum(joined_parts, axis=0))
    gain_first_grad = lax.optimization_barrier(jnp.sum(gain_one_parts, axis=0))
    joined_new, joined_momentum_new, joined_variance_new = adam_step(joined_proj, joined_grad, joined_momentum, joined_variance, WEIGHT_DECAY)
    out_new, out_momentum_new, out_variance_new = adam_step(out_proj, out_grad, out_momentum, out_variance, WEIGHT_DECAY)
    wide_new, wide_momentum_new, wide_variance_new = adam_step(wide_proj, wide_grad, wide_momentum, wide_variance, WEIGHT_DECAY)
    down_new, down_momentum_new, down_variance_new = adam_step(down_proj, down_grad, down_momentum, down_variance, WEIGHT_DECAY)
    gain_first_new, gain_first_momentum_new, gain_first_variance_new = adam_step(gain_first, gain_first_grad, gain_first_momentum, gain_first_variance, 0.0)
    gain_second_new, gain_second_momentum_new, gain_second_variance_new = adam_step(gain_second, gain_second_grad, gain_second_momentum, gain_second_variance, 0.0)
    return (output, stream_grad, joined_grad, out_grad, wide_grad, down_grad, gain_first_grad, gain_second_grad, joined_new, out_new, wide_new, down_new, gain_first_new, gain_second_new, joined_momentum_new, out_momentum_new, wide_momentum_new, down_momentum_new, gain_first_momentum_new, gain_second_momentum_new, joined_variance_new, out_variance_new, wide_variance_new, down_variance_new, gain_first_variance_new, gain_second_variance_new)
```

```python
import math

import jax
import jax.numpy as jnp
from jax import lax
from jax.sharding import PartitionSpec as P

HEAD_DIM = 64
LMAX = 1024
STEP = 4
GAIN_PAD = 384
OUT_PAD = 128


EPSILON = 1e-05
ROPE_BASE = 160000.0
LEARN_RATE = 0.02
BETA_ONE = 0.9
BETA_TWO = 0.98
ADAM_EPSILON = 1e-06
WEIGHT_DECAY = 0.1
NEG_LARGE = -1e30


def extended(x, sides, width):
    for axis, dim in sides:
        peers, length = (lax.axis_size(axis), x.shape[dim])
        up = [(i, (i + 1) % peers) for i in range(peers - 1)]
        down = [(j, i) for i, j in up]
        last = lax.slice_in_dim(x, length - width, length, axis=dim)
        initial = lax.slice_in_dim(x, 0, width, axis=dim)
        before = lax.ppermute(last, axis, up)
        after = lax.ppermute(initial, axis, down)
        x = jnp.concatenate([before, x, after], axis=dim)
    return x


def normalize(values):
    centred = values - jnp.mean(values, axis=1, keepdims=True)
    row_scale = lax.rsqrt(jnp.mean(centred * centred, axis=1, keepdims=True) + EPSILON)
    return (centred * row_scale, row_scale)


def norm_back(grad_hat, normed, row_scale):
    mean_one = jnp.mean(grad_hat, axis=1, keepdims=True)
    mean_two = jnp.mean(grad_hat * normed, axis=1, keepdims=True)
    return row_scale * (grad_hat - mean_one - normed * mean_two)


def rope_tables(positions):
    half_dim = HEAD_DIM // 2
    freqs = jnp.exp(
        jnp.arange(half_dim, dtype=jnp.float32) * (-2.0 * math.log(ROPE_BASE) / HEAD_DIM)
    )
    angles = positions.astype(jnp.float32)[:, None] * freqs[None, :]
    return (jnp.cos(angles), jnp.sin(angles))


def rotate(values, cosine, sine_table, sign):
    half_dim = values.shape[-1] // 2
    front_half = values[..., :half_dim]
    second = values[..., half_dim:]
    cos_part = cosine[:, None, :]
    sin_part = sine_table[:, None, :] * sign
    return jnp.concatenate(
        [front_half * cos_part - second * sin_part, second * cos_part + front_half * sin_part],
        axis=-1,
    )


def gelu_parts(inner_part):
    cdf_part = 0.5 * (1.0 + lax.erf(inner_part * (1.0 / math.sqrt(2.0))))
    activation = inner_part * cdf_part
    gelu_slope = cdf_part + inner_part * jnp.exp(-0.5 * inner_part * inner_part) * (
        1.0 / math.sqrt(2.0 * math.pi)
    )
    return (activation, gelu_slope)


def score_block(queries, win_keys, key_mask):
    scores = jnp.einsum(
        "rhd,khd->hrk", queries, win_keys, preferred_element_type=jnp.float32
    ) * HEAD_DIM ** (-0.5)
    return jnp.where(key_mask[None], scores, NEG_LARGE)


def attend_forward(queries, win_keys, win_values, key_mask):
    scores = score_block(queries, win_keys, key_mask)
    row_peak = jnp.max(scores, axis=2, keepdims=True)
    sum_exp = jnp.sum(jnp.exp(scores - row_peak), axis=2, keepdims=True)
    log_norm = row_peak + jnp.log(sum_exp)
    prob_round = jnp.exp(scores - log_norm).astype(jnp.bfloat16)
    mixed = jnp.einsum("hrk,khd->rhd", prob_round, win_values, preferred_element_type=jnp.float32)
    return (mixed, log_norm[..., 0])


def attend_backward(queries, win_keys, win_values, key_mask, log_norm, attended, grad_attended):
    scores = score_block(queries, win_keys, key_mask)
    probs = jnp.exp(scores - log_norm[..., None])
    prob_round = probs.astype(jnp.bfloat16)
    grad_prob = jnp.einsum(
        "rhd,khd->hrk", grad_attended, win_values, preferred_element_type=jnp.float32
    )
    row_delta = jnp.sum(grad_attended.astype(jnp.float32) * attended.astype(jnp.float32), axis=2).T
    grad_score = (probs * (grad_prob - row_delta[..., None])).astype(jnp.bfloat16)
    grad_query = jnp.einsum(
        "hrk,khd->rhd", grad_score, win_keys, preferred_element_type=jnp.float32
    ) * HEAD_DIM ** (-0.5)
    grad_key = jnp.einsum(
        "hrk,rhd->khd", grad_score, queries, preferred_element_type=jnp.float32
    ) * HEAD_DIM ** (-0.5)
    grad_value = jnp.einsum(
        "hrk,rhd->khd", prob_round, grad_attended, preferred_element_type=jnp.float32
    )
    return (grad_query, grad_key, grad_value)


def adam_step(weight, gradient, momentum, variance, decay_rate):
    new_momentum = BETA_ONE * momentum + (1.0 - BETA_ONE) * gradient
    new_variance = BETA_TWO * variance + (1.0 - BETA_TWO) * gradient * gradient
    update = (
        new_momentum
        / (1.0 - BETA_ONE**STEP)
        / (jnp.sqrt(new_variance / (1.0 - BETA_TWO**STEP)) + ADAM_EPSILON)
    )
    return (weight - LEARN_RATE * (update + decay_rate * weight), new_momentum, new_variance)


def scatter_sum(partial):
    moved = partial.astype(jnp.bfloat16)
    total = lax.psum_scatter(moved, ("dp", "group"), scatter_dimension=0, tiled=True)
    return total.astype(jnp.float32)


def with_column(matrix, column, extra):
    return jnp.concatenate([matrix, jnp.pad(column[:, None], ((0, 0), (0, extra - 1)))], axis=1)


def on_device(
    stream,
    cotangent,
    bounds,
    joined_proj,
    out_proj,
    wide_proj,
    down_proj,
    gain_first,
    gain_second,
    joined_momentum,
    out_momentum,
    wide_momentum,
    down_momentum,
    gain_first_momentum,
    gain_second_momentum,
    joined_variance,
    out_variance,
    wide_variance,
    down_variance,
    gain_first_variance,
    gain_second_variance,
):
    row_count = stream.shape[0]
    width = stream.shape[1]
    heads = width // HEAD_DIM
    both = ("dp", "group")
    gains = jnp.stack([gain_first, gain_second], axis=1)
    gains = jnp.pad(gains, ((0, 0), (0, GAIN_PAD - 2)))
    joined_gains = jnp.concatenate([joined_proj, gains], axis=1).astype(jnp.bfloat16)
    joined_gains = lax.all_gather(joined_gains, both, axis=0, tiled=True)
    joined_half = joined_gains[:, : 3 * width]
    gain_one_half = joined_gains[:, 3 * width]
    gain_two_half = joined_gains[:, 3 * width + 1]
    out_half = lax.all_gather(out_proj.astype(jnp.bfloat16), both, axis=0, tiled=True)
    wide_half = lax.all_gather(wide_proj.astype(jnp.bfloat16), both, axis=0, tiled=True)
    down_half = lax.all_gather(down_proj.astype(jnp.bfloat16), both, axis=0, tiled=True)
    gain_one = gain_one_half.astype(jnp.float32)
    gain_two = gain_two_half.astype(jnp.float32)
    ff_width = down_half.shape[1]
    first_row = lax.axis_index(("dp", "group")) * row_count
    token_index = first_row + jnp.arange(row_count, dtype=jnp.int32)
    seq_starts = bounds[:, 0]
    seq_ends = bounds[:, 1]
    cosine, sine_table = rope_tables(token_index - seq_starts)
    normed_one, scale_one = normalize(stream)
    normed_in = (normed_one * gain_one).astype(jnp.bfloat16)
    joined_act = jnp.dot(normed_in, joined_half, preferred_element_type=jnp.float32)
    queries = rotate(
        joined_act[:, :width].reshape(row_count, heads, HEAD_DIM), cosine, sine_table, 1.0
    ).astype(jnp.bfloat16)
    own_keys = rotate(
        joined_act[:, width : 2 * width].reshape(row_count, heads, HEAD_DIM),
        cosine,
        sine_table,
        1.0,
    )
    pairs = jnp.concatenate(
        [
            own_keys.astype(jnp.bfloat16).reshape(row_count, width),
            joined_act[:, 2 * width :].astype(jnp.bfloat16),
        ],
        axis=1,
    )
    key_span = row_count + 2 * LMAX
    group_block = lax.all_gather(pairs, "group", axis=0, tiled=True)
    padded = extended(group_block, (("dp", 0),), LMAX)
    window = lax.dynamic_slice_in_dim(padded, lax.axis_index("group") * row_count, key_span, 0)
    key_index = first_row - LMAX + jnp.arange(key_span, dtype=jnp.int32)
    key_mask = (key_index[None, :] >= seq_starts[:, None]) & (
        key_index[None, :] < seq_ends[:, None]
    )
    win_keys = window[:, :width].reshape(key_span, heads, HEAD_DIM)
    win_values = window[:, width:].reshape(key_span, heads, HEAD_DIM)
    mixed_parts = []
    norm_parts = []
    for head_start in range(0, heads, 4):
        mixed, log_norm = attend_forward(
            queries[:, head_start : head_start + 4],
            win_keys[:, head_start : head_start + 4],
            win_values[:, head_start : head_start + 4],
            key_mask,
        )
        mixed_parts.append(mixed)
        norm_parts.append(log_norm)
    attended = jnp.concatenate(mixed_parts, axis=1).astype(jnp.bfloat16).reshape(row_count, width)
    residual = stream + jnp.dot(attended, out_half, preferred_element_type=jnp.float32)
    normed_two, scale_two = normalize(residual)
    hidden_in = (normed_two * gain_two).astype(jnp.bfloat16)
    wide_act = jnp.dot(hidden_in, wide_half, preferred_element_type=jnp.float32)
    inner_part = wide_act[:, :ff_width]
    gate_part = wide_act[:, ff_width:]
    activation, gelu_slope = gelu_parts(inner_part)
    gated = (activation * gate_part).astype(jnp.bfloat16)
    output = residual + jnp.einsum(
        "rf,df->rd", gated, down_half, preferred_element_type=jnp.float32
    )
    cot_half = cotangent.astype(jnp.bfloat16)
    down_local = jnp.einsum("rd,rf->df", cot_half, gated, preferred_element_type=jnp.float32)
    grad_gated = jnp.dot(cot_half, down_half, preferred_element_type=jnp.float32)
    grad_inner = (grad_gated * gate_part * gelu_slope).astype(jnp.bfloat16)
    grad_gate = (grad_gated * activation).astype(jnp.bfloat16)
    grad_wide = jnp.concatenate([grad_inner, grad_gate], axis=1)
    down_sum = scatter_sum(down_local)
    inner_sum = scatter_sum(
        jnp.einsum("rd,rf->df", hidden_in, grad_inner, preferred_element_type=jnp.float32)
    )
    gate_sum = scatter_sum(
        jnp.einsum("rd,rf->df", hidden_in, grad_gate, preferred_element_type=jnp.float32)
    )
    grad_hidden = jnp.einsum("rf,df->rd", grad_wide, wide_half, preferred_element_type=jnp.float32)
    gain_two_local = jnp.sum(grad_hidden * normed_two, axis=0)
    grad_resid = cotangent + norm_back(grad_hidden * gain_two, normed_two, scale_two)
    resid_half = grad_resid.astype(jnp.bfloat16)
    out_local = jnp.einsum("rd,re->de", attended, resid_half, preferred_element_type=jnp.float32)
    out_sum = scatter_sum(with_column(out_local, gain_two_local, OUT_PAD))
    grad_attended = jnp.einsum(
        "re,de->rd", resid_half, out_half, preferred_element_type=jnp.float32
    ).astype(jnp.bfloat16)
    attended_heads = attended.reshape(row_count, heads, HEAD_DIM)
    grad_heads = grad_attended.reshape(row_count, heads, HEAD_DIM)
    query_parts = []
    key_parts = []
    value_parts = []
    for part_index, head_start in enumerate(range(0, heads, 4)):
        grad_query, grad_key, grad_value = attend_backward(
            queries[:, head_start : head_start + 4],
            win_keys[:, head_start : head_start + 4],
            win_values[:, head_start : head_start + 4],
            key_mask,
            norm_parts[part_index],
            attended_heads[:, head_start : head_start + 4],
            grad_heads[:, head_start : head_start + 4],
        )
        query_parts.append(grad_query)
        key_parts.append(grad_key)
        value_parts.append(grad_value)
    grad_queries = jnp.concatenate(query_parts, axis=1)
    grad_window = jnp.concatenate(
        [
            jnp.concatenate(key_parts, axis=1).reshape(key_span, width),
            jnp.concatenate(value_parts, axis=1).reshape(key_span, width),
        ],
        axis=1,
    )
    block_rows = row_count * lax.axis_size("group")
    holder = jnp.zeros((block_rows + 2 * LMAX, 2 * width), jnp.bfloat16)
    holder = lax.dynamic_update_slice_in_dim(
        holder, grad_window.astype(jnp.bfloat16), lax.axis_index("group") * row_count, 0
    )
    rim_rows = jnp.concatenate([holder[:LMAX], holder[block_rows + LMAX :]], axis=0)
    moved = extended(rim_rows, (("dp", 0),), LMAX).astype(jnp.float32)
    centre = holder[LMAX : LMAX + block_rows].astype(jnp.float32)
    centre = centre.at[:LMAX].add(moved[:LMAX])
    centre = centre.at[block_rows - LMAX :].add(moved[3 * LMAX :])
    pair_grad = lax.psum_scatter(
        centre.astype(jnp.bfloat16), "group", scatter_dimension=0, tiled=True
    ).astype(jnp.float32)
    query_back = rotate(grad_queries, cosine, sine_table, -1.0).reshape(row_count, width)
    key_back = rotate(
        pair_grad[:, :width].reshape(row_count, heads, HEAD_DIM), cosine, sine_table, -1.0
    )
    grad_joined = jnp.concatenate(
        [query_back, key_back.reshape(row_count, width), pair_grad[:, width:]], axis=1
    ).astype(jnp.bfloat16)
    joined_local = jnp.einsum(
        "rd,re->de", normed_in, grad_joined, preferred_element_type=jnp.float32
    )
    grad_normed = jnp.einsum(
        "re,de->rd", grad_joined, joined_half, preferred_element_type=jnp.float32
    )
    gain_one_local = jnp.sum(grad_normed * normed_one, axis=0)
    stream_grad = grad_resid + norm_back(grad_normed * gain_one, normed_one, scale_one)
    joined_sum = scatter_sum(with_column(joined_local, gain_one_local, GAIN_PAD))
    joined_grad = joined_sum[:, : 3 * width]
    gain_first_grad = joined_sum[:, 3 * width]
    out_grad = out_sum[:, :width]
    gain_second_grad = out_sum[:, width]
    wide_grad = jnp.concatenate([inner_sum, gate_sum], axis=1)
    down_grad = down_sum
    joined_new, joined_momentum_new, joined_variance_new = adam_step(
        joined_proj, joined_grad, joined_momentum, joined_variance, WEIGHT_DECAY
    )
    out_new, out_momentum_new, out_variance_new = adam_step(
        out_proj, out_grad, out_momentum, out_variance, WEIGHT_DECAY
    )
    wide_new, wide_momentum_new, wide_variance_new = adam_step(
        wide_proj, wide_grad, wide_momentum, wide_variance, WEIGHT_DECAY
    )
    down_new, down_momentum_new, down_variance_new = adam_step(
        down_proj, down_grad, down_momentum, down_variance, WEIGHT_DECAY
    )
    gain_first_new, gain_first_momentum_new, gain_first_variance_new = adam_step(
        gain_first, gain_first_grad, gain_first_momentum, gain_first_variance, 0.0
    )
    gain_second_new, gain_second_momentum_new, gain_second_variance_new = adam_step(
        gain_second, gain_second_grad, gain_second_momentum, gain_second_variance, 0.0
    )
    return (
        output,
        stream_grad,
        joined_grad,
        out_grad,
        wide_grad,
        down_grad,
        gain_first_grad,
        gain_second_grad,
        joined_new,
        out_new,
        wide_new,
        down_new,
        gain_first_new,
        gain_second_new,
        joined_momentum_new,
        out_momentum_new,
        wide_momentum_new,
        down_momentum_new,
        gain_first_momentum_new,
        gain_second_momentum_new,
        joined_variance_new,
        out_variance_new,
        wide_variance_new,
        down_variance_new,
        gain_first_variance_new,
        gain_second_variance_new,
    )


def solution(mesh):
    placed = (
        P(("dp", "group"), None),
        P(("dp", "group"), None),
        P(("dp", "group"), None),
        P(("dp", "group"), None),
        P(("dp", "group"), None),
        P(("dp", "group"), None),
        P(("dp", "group"), None),
        P(("dp", "group")),
        P(("dp", "group")),
        P(("dp", "group"), None),
        P(("dp", "group"), None),
        P(("dp", "group"), None),
        P(("dp", "group"), None),
        P(("dp", "group")),
        P(("dp", "group")),
        P(("dp", "group"), None),
        P(("dp", "group"), None),
        P(("dp", "group"), None),
        P(("dp", "group"), None),
        P(("dp", "group")),
        P(("dp", "group")),
    )
    return jax.shard_map(
        on_device,
        mesh=mesh,
        in_specs=placed,
        out_specs=(
            P(("dp", "group"), None),
            P(("dp", "group"), None),
            P(("dp", "group"), None),
            P(("dp", "group"), None),
            P(("dp", "group"), None),
            P(("dp", "group"), None),
            P(("dp", "group")),
            P(("dp", "group")),
            P(("dp", "group"), None),
            P(("dp", "group"), None),
            P(("dp", "group"), None),
            P(("dp", "group"), None),
            P(("dp", "group")),
            P(("dp", "group")),
            P(("dp", "group"), None),
            P(("dp", "group"), None),
            P(("dp", "group"), None),
            P(("dp", "group"), None),
            P(("dp", "group")),
            P(("dp", "group")),
            P(("dp", "group"), None),
            P(("dp", "group"), None),
            P(("dp", "group"), None),
            P(("dp", "group"), None),
            P(("dp", "group")),
            P(("dp", "group")),
        ),
        check_vma=False,
    )
```
